32 devices in a mesh: aper: 8 (over y, x, core), swath: 4 (over z).
Axes of the slice: x: 2, y: 2, z: 4, core: 2. Of those that a mesh axis runs over, the one named last changes fastest.
Arguments:
- polar_field: float32 [2, 1024, 4096], P(None, 'aper', 'swath'), may hold values from -6 to 6
- tap_index: int32 [3, 8, 2, 8, 128], P(None, 'aper'), may hold values from 0 to 127
- tap_weight: float32 [3, 8, 2, 8, 128], P(None, 'aper'), may hold values from -1.5 to 1.5
- range_shift: float32 [3, 8, 2, 128], P(None, 'aper'), may hold values from -8 to 8
- range_gain: float32 [3, 4096], P(None, 'swath'), may hold values from 0.1 to 1.9
- tile_owner: int32 [8, 4, 8, 1], P('aper', 'swath'), may hold values from 0 to 7; in each aligned block of 8 rows (0 to 7, 8 to 15, ..., all dimensions but the last counted through in order) at most 2 rows name the same one
- block_weights: float32 [8, 4, 8, 128, 128], P('aper', 'swath'), may hold values from -0.5 to 0.5
- kernel_index: int32 [8, 4], P('aper', 'swath'), may hold values from 0 to 15
- kernel_bank: float32 [16, 81], replicated, may hold values from -0.625 to 0.625
Outputs:
- deconvolved: float32 [2, 1024, 512], P(None, 'aper', 'swath')
The draws below stay inside these ranges and needn't reach their ends.
Inputs may be any that keep to these rules, and one draw needn't show every extreme that they name: `tile_owner`: the 8 polar blocks of one device name any one owner at most 2 times, and some device names one owner exactly 2 times; every owner is named somewhere.
All inputs are finite; a program needn't handle non-finite values.
Results may differ from the reference program's by a relative error of at most 0.00011.
Values sent between devices are 32-bit elements; how exact they have to be, the bound alone decides.
A program may use at most 128 MiB of HBM per device.

```python
import math
import jax
import jax.numpy as jnp
import numpy as np
from jax import lax

ANGLES = 128
RANGE_BINS = 1024
TAPS = 8
SECTIONS = 3
BLOCK_BINS = 128
TILE_ROWS = 128
SLOTS = 2
KERNELS = 16
N_APER = 8
N_SWATH = 4


def with_ends(values, rng, least, high):
    longest = values.shape.index(max(values.shape))
    spots = []
    for shift in (0, 1):
        where = [jax.random.randint(jax.random.fold_in(rng, axis), (), 0, length) for axis, length in enumerate(values.shape)]
        where[longest] = (where[longest] + shift) % values.shape[longest]
        spots.append(tuple(where))
    return values.at[spots[0]].set(least).at[spots[1]].set(high)


def block_levels(key, extent, shards, smallest, top_value):
    gain, own = 1.0, jax.random.fold_in(key, 6)
    for axis_at, blocks in shards:
        steps = jnp.exp(jax.random.uniform(jax.random.fold_in(own, axis_at), (blocks,), jnp.float32, smallest / len(shards), top_value / len(shards)))
        gain = gain * jnp.repeat(steps, extent[axis_at] // blocks).reshape([-1 if axis == axis_at else 1 for axis in range(len(extent))])
    return gain


def shared_out(stream_key, own, number, rows, amount, top, reach, slope):
    order = jax.random.permutation(stream_key, amount)
    crowded, ordinary = load_shares(amount, rows * top, reach, slope, True), load_shares(amount, rows * top, reach, slope, False)
    places = jnp.arange(amount)

    def named(lengths, rotation):
        used = int((lengths > 0).sum())
        fixed = max(1, used // 4)
        passed = fixed + (places - fixed + rotation * (used - fixed)) % max(1, amount - fixed)
        return jnp.zeros((amount,), jnp.int32).at[order[jnp.where(places < fixed, places, passed)]].set(jnp.asarray(lengths, jnp.int32))

    lengths = jnp.where(number % 4 == 0, named(crowded, number // 4), named(ordinary, number - number // 4 - 1))
    mixed = jax.random.permutation(jax.random.fold_in(own, 3), amount)
    source_of, taker = mixed[0:amount // 2 * 2:2], mixed[1:amount // 2 * 2:2]
    margin = jnp.minimum(lengths[source_of] - 1, reach - lengths[taker]) // 2
    margin = jnp.where((source_of == order[0]) | (taker == order[0]) | (lengths[taker] == 0), 0, jnp.maximum(margin, 0))
    passed = jax.random.randint(jax.random.fold_in(own, 4), (amount // 2,), 0, 1 << 20) % (margin + 1)
    lengths = lengths.at[source_of].add(-passed).at[taker].add(passed)
    members = jnp.searchsorted(jnp.cumsum(lengths), jnp.arange(rows * top), side="right").astype(jnp.int32)
    grid = members.reshape(top, rows).T
    grid = grid[jax.random.permutation(jax.random.fold_in(own, 1), rows)]
    rotation = jax.random.randint(jax.random.fold_in(own, 2), (rows, 1), 0, top)
    return jnp.take_along_axis(grid, (jnp.arange(top)[None, :] + rotation) % top, axis=1)


def load_shares(number_of, total, limit, slope, full):
    weights = [(1 << 20) // math.isqrt(rank ** slope) + 1 for rank in range(1, number_of + 1)]
    largest = limit if full else min(limit, max(-(-total // number_of), total * weights[0] // sum(weights)))
    least = 1 if total - largest >= number_of - 1 else 0
    given, rest = [largest] + [least] * (number_of - 1), total - largest - least * (number_of - 1)
    while rest > 0:
        candidates = [i for i in range(1, number_of) if given[i] < largest] or [i for i in range(1, number_of) if given[i] < limit]
        pool, left = sum([weights[i] for i in candidates]), rest
        for i in candidates:
            more = min(limit - given[i], max(1, left * weights[i] // pool), rest)
            given[i] = given[i] + more
            rest = rest - more
    return np.array(given)


def scatter_about(key, extent, spread, bound, split=(), held_as=jnp.bfloat16):
    drawn = jax.random.normal(key, extent, jnp.float32) * spread
    if len(split) > 0:
        drawn = block_levels(key, extent, split, -0.22, 0.18) * drawn
    return jnp.clip(drawn, min=-bound, max=bound).astype(held_as)


def setup_inputs(seed: int = 0) -> dict:
    splits = jax.random.split(jax.random.key(seed), 10)
    polar_field = scatter_about(splits[0], (2, ANGLES * N_APER, RANGE_BINS * N_SWATH), 1.0, 6.0, ((1, 8), (2, 4)), jnp.float32)
    tap_index = with_ends(jax.random.randint(splits[1], (SECTIONS, N_APER, 2, TAPS, ANGLES), 0, ANGLES), jax.random.fold_in(splits[1], 1), 0, ANGLES - 1).astype(jnp.int32)
    tap_weight = scatter_about(splits[2], (SECTIONS, N_APER, 2, TAPS, ANGLES), 0.25, 1.5, ((1, 8),), jnp.float32)
    range_shift = jnp.clip(jax.random.uniform(splits[3], (SECTIONS, N_APER, 2, ANGLES), jnp.float32, -8.0, 8.0) * block_levels(splits[3], (SECTIONS, N_APER, 2, ANGLES), ((1, 8),), -0.4, 0.0), -8.0, 8.0)
    range_gain = jnp.clip(1.0 + 0.18 * jax.random.normal(splits[4], (SECTIONS, RANGE_BINS * N_SWATH), jnp.float32), 0.1, 1.9)
    tile_owner_keys = jax.random.split(jax.random.fold_in(splits[5], 1), N_APER * N_SWATH * (RANGE_BINS // BLOCK_BINS) // (RANGE_BINS // BLOCK_BINS))
    tile_owner_turns = jax.random.permutation(jax.random.fold_in(splits[5], 3), N_APER * N_SWATH * (RANGE_BINS // BLOCK_BINS) // (RANGE_BINS // BLOCK_BINS))
    tile_owner = jax.vmap(lambda own, number: shared_out(jax.random.fold_in(splits[5], 2), own, number, RANGE_BINS // BLOCK_BINS, N_APER, 1, SLOTS, 2))(tile_owner_keys, tile_owner_turns).reshape((N_APER, N_SWATH, RANGE_BINS // BLOCK_BINS, 1))
    block_weights = scatter_about(splits[6], (N_APER, N_SWATH, RANGE_BINS // BLOCK_BINS, TILE_ROWS, ANGLES), ANGLES ** -0.5, 0.5, ((0, 8), (1, 4)), jnp.float32)
    kernel_index = with_ends(jax.random.randint(splits[7], (N_APER, N_SWATH), 0, KERNELS), jax.random.fold_in(splits[7], 1), 0, KERNELS - 1).astype(jnp.int32)
    kernel_bank = scatter_about(splits[8], (KERNELS, 81), 81 ** -0.5, 0.625, (), jnp.float32)
    return {"polar_field": polar_field, "tap_index": tap_index, "tap_weight": tap_weight, "range_shift": range_shift, "range_gain": range_gain, "tile_owner": tile_owner, "block_weights": block_weights, "kernel_index": kernel_index, "kernel_bank": kernel_bank}


HIGHEST_PRECISION = lax.Precision.HIGHEST


def transform_tables(length):
    bin_index = jnp.arange(length, dtype=jnp.int32)
    product = (bin_index[:, None] * bin_index[None, :]) % length
    phase_angle = product.astype(jnp.float32) * jnp.float32(2.0 * math.pi / length)
    return jnp.cos(phase_angle), jnp.sin(phase_angle)


def forward(signal, cos_table, sin_table):
    with_cos = jnp.dot(signal, cos_table, precision=HIGHEST_PRECISION, preferred_element_type=jnp.float32)
    with_sin = jnp.dot(signal, sin_table, precision=HIGHEST_PRECISION, preferred_element_type=jnp.float32)
    return jnp.stack([with_cos[0] + with_sin[1], with_cos[1] - with_sin[0]])


def inverse(signal, cos_table, sin_table):
    length = cos_table.shape[0]
    with_cos = jnp.dot(signal, cos_table, precision=HIGHEST_PRECISION, preferred_element_type=jnp.float32)
    with_sin = jnp.dot(signal, sin_table, precision=HIGHEST_PRECISION, preferred_element_type=jnp.float32)
    return jnp.stack([(with_cos[0] - with_sin[1]) / length, (with_cos[1] + with_sin[0]) / length])


def interp_matrix(tap_rows, weight_rows, length):
    columns = jnp.arange(length, dtype=jnp.int32)
    matches = (tap_rows[..., None] == columns).astype(jnp.float32)
    return jnp.sum(weight_rows[..., None] * matches, axis=-3)


def phase_tables(shift_rows, length):
    bin_index = jnp.arange(length, dtype=jnp.int32)
    signed = jnp.where(bin_index < length // 2, bin_index, bin_index - length).astype(jnp.float32)
    phase_angle = shift_rows[..., None] * signed * jnp.float32(-2.0 * math.pi / length)
    return jnp.cos(phase_angle), jnp.sin(phase_angle)


def steer_all(matrix, shift_rows, spectra):
    mixed = jnp.einsum("ikj,pijbr->pikbr", matrix.astype(jnp.float32), spectra.astype(jnp.float32), precision=HIGHEST_PRECISION)
    cos_phase, sin_phase = phase_tables(shift_rows, RANGE_BINS)
    cos_phase = cos_phase[:, :, None, :]
    sin_phase = sin_phase[:, :, None, :]
    return jnp.stack([cos_phase * mixed[0] - sin_phase * mixed[1], cos_phase * mixed[1] + sin_phase * mixed[0]])


def reference(polar_field, tap_index, tap_weight, range_shift, range_gain, tile_owner, block_weights, kernel_index, kernel_bank):
    cos_table, sin_table = transform_tables(RANGE_BINS)
    current = polar_field.reshape(2, N_APER, ANGLES, N_SWATH, RANGE_BINS)
    gain_rows = range_gain.reshape(SECTIONS, N_SWATH, RANGE_BINS)
    devices = np.arange(N_APER)
    for merge_step in range(SECTIONS):
        spectra = forward(current, cos_table, sin_table)
        matrices = interp_matrix(tap_index[merge_step], tap_weight[merge_step], ANGLES)
        lower_child = devices & ~(1 << merge_step)
        upper_child = devices | (1 << merge_step)
        merged = steer_all(matrices[:, 0], range_shift[merge_step][:, 0], spectra[:, lower_child])
        merged = merged + steer_all(matrices[:, 1], range_shift[merge_step][:, 1], spectra[:, upper_child])
        current = inverse(merged, cos_table, sin_table) * gain_rows[merge_step][None, None, None, :, :]
    blocks_dev = RANGE_BINS // BLOCK_BINS
    pieces = current.reshape(2, N_APER, ANGLES, N_SWATH, blocks_dev, BLOCK_BINS)
    contrib = jnp.einsum("asbxk,paksby->asbpxy", block_weights.astype(jnp.float32), pieces, precision=HIGHEST_PRECISION)
    owner_ids = tile_owner[..., 0]
    owner_hits = (owner_ids[..., None] == jnp.arange(N_APER, dtype=jnp.int32)).astype(jnp.float32)
    tile_grid = jnp.einsum("asbd,asbpxy->dspxy", owner_hits, contrib, precision=HIGHEST_PRECISION)
    cart_image = tile_grid.transpose(2, 0, 3, 1, 4).reshape(2, N_APER * TILE_ROWS, N_SWATH * BLOCK_BINS)
    padded = jnp.pad(cart_image, ((0, 0), (4, 4), (4, 4)))
    chosen = kernel_bank[kernel_index]
    result_sum = jnp.zeros((2, N_APER, TILE_ROWS, N_SWATH, BLOCK_BINS), jnp.float32)
    for offset in range(81):
        row_shift = offset // 9
        col_shift = offset % 9
        window = padded[:, row_shift:row_shift + N_APER * TILE_ROWS, col_shift:col_shift + N_SWATH * BLOCK_BINS]
        window = window.reshape(2, N_APER, TILE_ROWS, N_SWATH, BLOCK_BINS)
        result_sum = result_sum + chosen[:, :, offset][None, :, None, :, None] * window
    return result_sum.reshape(2, N_APER * TILE_ROWS, N_SWATH * BLOCK_BINS)
```

```python
import functools
import math

import jax
import jax.numpy as jnp
import numpy as np
from jax import lax
from jax.experimental import pallas as pl
from jax.experimental.pallas import tpu as pltpu
from jax.sharding import PartitionSpec as P

ANGLES = 128
RANGE_BINS = 1024
LANES = 128
GROUPS = RANGE_BINS // LANES
WIDE = 2 * LANES
TILE_ROWS = 128
TAPS = 8
CHUNKS = 4
ROWS = ANGLES // CHUNKS
EDGE = 8
REACH = 4
MESH = pl.DeviceIdType.MESH
F32 = jnp.float32
BF16 = jnp.bfloat16


def split(value):
    high = value.astype(BF16)
    return high, (value - high.astype(F32)).astype(BF16)


def product(left, right):
    def dot(a, b):
        return jnp.dot(a, b, preferred_element_type=F32)

    return dot(left[0], right[0]) + dot(left[1], right[0]) + dot(left[0], right[1])


def turn(value):
    half = (value - jnp.floor(value + 0.5)) * F32(math.pi)
    square = half * half
    sine = F32(-1.0 / math.factorial(15))
    for order in (13, 11, 9, 7, 5, 3, 1):
        sign = 1.0 if order % 4 == 1 else -1.0
        sine = sine * square + F32(sign / math.factorial(order))
    sine = sine * half
    cosine = F32(1.0 / math.factorial(16))
    for order in (14, 12, 10, 8, 6, 4, 2, 0):
        sign = 1.0 if order % 4 == 0 else -1.0
        cosine = cosine * square + F32(sign / math.factorial(order))
    return 1.0 - 2.0 * sine * sine, 2.0 * sine * cosine


def four(x):
    (ar, ai), (br, bi), (cr, ci), (dr, di) = x
    sr, si, tr, ti = ar + cr, ai + ci, ar - cr, ai - ci
    ur, ui, vr, vi = br + dr, bi + di, br - dr, bi - di
    return [(sr + ur, si + ui), (tr + vi, ti - vr), (sr - ur, si - ui), (tr - vi, ti + vr)]


def eight(x):
    even, odd = four(x[0::2]), four(x[1::2])
    root = F32(math.sqrt(0.5))
    turned = [
        odd[0],
        ((odd[1][0] + odd[1][1]) * root, (odd[1][1] - odd[1][0]) * root),
        (odd[2][1], -odd[2][0]),
        ((odd[3][1] - odd[3][0]) * root, -(odd[3][0] + odd[3][1]) * root),
    ]
    first = [(e[0] + o[0], e[1] + o[1]) for e, o in zip(even, turned)]
    return first + [(e[0] - o[0], e[1] - o[1]) for e, o in zip(even, turned)]


def twiddle(pairs, cos_ref, sin_ref):
    out = [pairs[0]]
    for group in range(1, GROUPS):
        a, b = pairs[group]
        c, s = cos_ref[group : group + 1, :], sin_ref[group : group + 1, :]
        out.append((a * c + b * s, b * c - a * s))
    return out


def short_dft(pairs, table):
    rows = pairs[0][0].shape[0]
    stacked = jnp.concatenate([jnp.concatenate(pair, axis=1) for pair in pairs], axis=0)
    out = product(split(stacked), table)
    return [out[g * rows : (g + 1) * rows] for g in range(len(pairs))]


def forward(pairs, table, cos_ref, sin_ref):
    return short_dft(twiddle(eight(pairs), cos_ref, sin_ref), table)


def inverse(merged, table, cos_ref, sin_ref, gain):
    out = short_dft([(im, re) for re, im in merged], table)
    pairs = eight(twiddle([(o[:, :LANES], o[:, LANES:]) for o in out], cos_ref, sin_ref))
    scaled = gain * F32(1.0 / RANGE_BINS)
    result = []
    for group, (im, re) in enumerate(pairs):
        weight = scaled[:, group * LANES : (group + 1) * LANES]
        result.append((re * weight, im * weight))
    return result


def kernel(
    peers,
    swaths,
    sections,
    polar,
    taps,
    weights,
    shifts,
    gains,
    owner,
    block_weights,
    kernel_index,
    bank,
    table_high,
    table_low,
    cos_ref,
    sin_ref,
    result,
    matrix,
    phases,
    spec0,
    spec1,
    spec2,
    got0,
    got1,
    got2,
    mixed,
    total,
    image,
    mat_send,
    mat_got,
    part,
    part_got,
    row_halo,
    col_halo,
    flipped,
    shifted,
    send_sem,
    recv_sem,
    mat_sem,
    part_send,
    part_recv,
    halo_send,
    halo_recv,
):
    me = lax.axis_index("aper")
    column = lax.axis_index("swath")
    levels = peers.bit_length() - 1

    row_halo[...] = jnp.zeros_like(row_halo)
    col_halo[...] = jnp.zeros_like(col_halo)

    around = [(da, ds) for da in (-1, 0, 1) for ds in (-1, 0, 1) if (da, ds) != (0, 0)]
    barrier = pltpu.get_barrier_semaphore()
    for level in range(levels):
        pl.semaphore_signal(
            barrier, inc=1, device_id=(me ^ (1 << level), column), device_id_type=MESH
        )
    for da, ds in around:
        where = (lax.rem(me + da + peers, peers), lax.rem(column + ds + swaths, swaths))
        pl.semaphore_signal(barrier, inc=1, device_id=where, device_id_type=MESH)

    bits = [lax.rem(me // (1 << step), 2) for step in range(levels)]
    table = (table_high[...], table_low[...])

    def interp(step, child):
        index = taps[step, 0, child]
        weight = weights[step, 0, child]
        rows = lax.broadcasted_iota(jnp.int32, (ANGLES, ANGLES), 0)
        built = jnp.zeros((ANGLES, ANGLES), F32)
        for tap in range(TAPS):
            built = built + jnp.where(
                index[tap : tap + 1, :] == rows, weight[tap : tap + 1, :], F32(0.0)
            )
        return built.T

    def fill_phases(step, side, child):
        row = shifts[step, 0, pl.ds(child, 1), :]
        shift = jnp.broadcast_to(row, (ANGLES, LANES)).T
        lane = lax.broadcasted_iota(jnp.int32, (ANGLES, LANES), 1)
        signed = jnp.where(lane < LANES // 2, lane, lane - LANES).astype(F32)
        unit = shift * F32(-1.0 / RANGE_BINS)
        step_cos, step_sin = turn(unit)
        a, b = turn(unit * (signed * F32(GROUPS)))
        for group in range(GROUPS):
            phases[step, side, group, 0] = a
            phases[step, side, group, 1] = b
            if group + 1 < GROUPS:
                a, b = a * step_cos - b * step_sin, b * step_cos + a * step_sin

    def steered(step, side, group, rows, value):
        a = phases[step, side, group, 0, rows, :]
        b = phases[step, side, group, 1, rows, :]
        re, im = value[:, :LANES], value[:, LANES:]
        return jnp.concatenate([a * re - b * im, b * re + a * im], axis=1)

    def lanes(group):
        return slice(group * WIDE, (group + 1) * WIDE)

    def chunk(k):
        return slice(k * ROWS, (k + 1) * ROWS)

    def exchange(step, k, source, target):
        return pltpu.make_async_remote_copy(
            src_ref=source.at[pl.ds(k * ROWS, ROWS)],
            dst_ref=target.at[pl.ds(k * ROWS, ROWS)],
            send_sem=send_sem.at[step, k],
            recv_sem=recv_sem.at[step, k],
            device_id=(me ^ (1 << step), column),
            device_id_type=MESH,
        )

    def store_wide(target, rows, values):
        for group in range(GROUPS):
            target[rows, lanes(group)] = values[group]

    def merged_rows(rows):
        pairs = []
        for group in range(GROUPS):
            value = total[rows, lanes(group)]
            pairs.append((value[:, :LANES], value[:, LANES:]))
        return pairs

    everything = slice(0, ANGLES)

    copies0 = []
    for k in range(CHUNKS):
        rows = chunk(k)
        pairs = [
            (polar[0, rows, g * LANES : (g + 1) * LANES], polar[1, rows, g * LANES : (g + 1) * LANES])
            for g in range(GROUPS)
        ]
        store_wide(spec0, rows, forward(pairs, table, cos_ref, sin_ref))
        if k == 0:
            pl.semaphore_wait(barrier, levels + len(around))
        copies0.append(exchange(0, k, spec0, got0))
        copies0[-1].start()
    mat_send[...] = interp(1, 1 - bits[1])
    mat_copy = pltpu.make_async_remote_copy(
        src_ref=mat_send,
        dst_ref=mat_got,
        send_sem=mat_sem.at[0],
        recv_sem=mat_sem.at[1],
        device_id=(me ^ 2, column),
        device_id_type=MESH,
    )
    mat_copy.start()
    fill_phases(0, 0, bits[0])
    fill_phases(0, 1, 1 - bits[0])

    def mix(step, side, source, first):
        left = split(interp(step, bits[step] if side == 0 else 1 - bits[step]))
        for group in range(GROUPS):
            value = product(left, split(source[:, lanes(group)]))
            value = steered(step, side, group, everything, value)
            if not first:
                value = value + total[:, lanes(group)]
            total[:, lanes(group)] = value

    mix(0, 0, spec0, True)
    for copy in copies0:
        copy.wait()
    mix(0, 1, got0, False)
    for k in range(CHUNKS):
        rows = chunk(k)
        pairs = inverse(merged_rows(rows), table, cos_ref, sin_ref, gains[0:1, :])
        store_wide(spec1, rows, forward(pairs, table, cos_ref, sin_ref))

    mat_copy.wait()
    copies1 = []
    for k in range(CHUNKS):
        rows = chunk(k)
        left = split(mat_got[rows, :])
        for group in range(GROUPS):
            mixed[rows, lanes(group)] = product(left, split(spec1[:, lanes(group)]))
        copies1.append(exchange(1, k, mixed, got1))
        copies1[-1].start()
    fill_phases(1, 0, bits[1])
    fill_phases(1, 1, 1 - bits[1])
    mix(1, 0, spec1, True)
    copies2 = []
    for k in range(CHUNKS):
        rows = chunk(k)
        copies1[k].wait()
        pairs = []
        for group in range(GROUPS):
            value = total[rows, lanes(group)] + steered(
                1, 1, group, rows, got1[rows, lanes(group)]
            )
            pairs.append((value[:, :LANES], value[:, LANES:]))
        pairs = inverse(pairs, table, cos_ref, sin_ref, gains[1:2, :])
        store_wide(spec2, rows, forward(pairs, table, cos_ref, sin_ref))
        copies2.append(exchange(2, k, spec2, got2))
        copies2[-1].start()
        if k == 0:
            fill_phases(2, 0, bits[2])
            fill_phases(2, 1, 1 - bits[2])

    mix(2, 0, spec2, True)
    for copy in copies2:
        copy.wait()
    mix(2, 1, got2, False)
    for k in range(CHUNKS):
        rows = chunk(k)
        pairs = inverse(merged_rows(rows), table, cos_ref, sin_ref, gains[2:3, :])
        store_wide(image, rows, [jnp.concatenate(pair, axis=1) for pair in pairs])

    for q in range(GROUPS):
        matrix[q] = product(split(block_weights[0, 0, q]), split(image[:, lanes(q)]))

    def gathered(d):
        value = None
        for q in range(GROUPS):
            hit = jnp.where(owner[q] == d, F32(1.0), F32(0.0))
            value = hit * matrix[q] if value is None else value + hit * matrix[q]
        return value

    def part_copy(level, slot, source, target):
        return pltpu.make_async_remote_copy(
            src_ref=source,
            dst_ref=target,
            send_sem=part_send.at[slot],
            recv_sem=part_recv.at[slot],
            device_id=(me ^ (1 << level), column),
            device_id_type=MESH,
        )

    half = peers // 2
    copies = []
    for d in range(half):
        part[half + d] = gathered(2 * d + 1 - bits[0])
        copies.append(part_copy(0, d, part.at[half + d], part_got.at[d]))
        copies[-1].start()
    for d in range(half):
        part[d] = gathered(2 * d + bits[0])
    for d in range(half):
        copies[d].wait()
        part[d] = part[d] + part_got[d]
    base, here = half, 0
    count = half
    for level in range(1, levels):
        count = count // 2
        copies = []
        for d in range(count):
            copies.append(
                part_copy(
                    level,
                    base + d,
                    part.at[here + 2 * d + 1 - bits[level]],
                    part_got.at[base + d],
                )
            )
            copies[-1].start()
        after = peers + base - half
        for d in range(count):
            copies[d].wait()
            part[after + d] = part[here + 2 * d + bits[level]] + part_got[base + d]
        here = after
        base = base + count
    tile = part.at[here]

    for plane in range(2):
        flipped[plane] = tile[:, plane * LANES : (plane + 1) * LANES].T

    def halo_copy(da, ds):
        slot = [r for r in range(len(around)) if around[r] == (-da, -ds)][0]
        if da != 0:
            edge = 0 if da < 0 else TILE_ROWS - EDGE
            source = tile.at[pl.ds(edge, EDGE)]
            target = row_halo.at[1 if da < 0 else 0, 1 - ds]
        else:
            edge = 0 if ds < 0 else LANES - EDGE
            source = flipped.at[:, pl.ds(edge, EDGE)]
            target = col_halo.at[1 if ds < 0 else 0]
        return pltpu.make_async_remote_copy(
            src_ref=source,
            dst_ref=target,
            send_sem=halo_send.at[slot],
            recv_sem=halo_recv.at[slot],
            device_id=(me + da, column + ds),
            device_id_type=MESH,
        )

    def present(da, ds):
        found = None
        for place, step, extent in ((me, da, peers), (column, ds, swaths)):
            if step != 0:
                inside = place > 0 if step < 0 else place < extent - 1
                found = inside if found is None else jnp.logical_and(found, inside)
        return found

    for da, ds in around:

        @pl.when(present(da, ds))
        def _(da=da, ds=ds):
            halo_copy(da, ds).start()

    for da, ds in around:

        @pl.when(present(da, ds))
        def _(da=da, ds=ds):
            halo_copy(da, ds).wait_send()
            halo_copy(-da, -ds).wait_recv()

    lane = lax.broadcasted_iota(jnp.int32, (EDGE, LANES), 1)
    chosen = kernel_index[0]
    gap = jnp.zeros((LANES - 2 * EDGE, LANES), F32)
    for plane in range(2):
        cut = slice(plane * LANES, (plane + 1) * LANES)

        def strip(end):
            side = jnp.where(
                lane < LANES // 2, row_halo[end, 2, :, cut], row_halo[end, 0, :, cut]
            )
            return jnp.concatenate([row_halo[end, 1, :, cut], side], axis=1)

        side = jnp.concatenate([col_halo[1, plane], gap, col_halo[0, plane]], axis=0).T
        middle = jnp.concatenate([tile[:, cut], side], axis=1)
        whole = jnp.concatenate([strip(0), middle, strip(1)], axis=0)
        summed = jnp.zeros((TILE_ROWS, LANES), F32)
        for v in range(2 * REACH + 1):
            moved = whole if v == REACH else pltpu.roll(whole, (REACH - v) % WIDE, 1)
            shifted[v] = moved[:, :LANES]
            for u in range(2 * REACH + 1):
                start = EDGE - REACH + u
                summed = (
                    summed
                    + bank[chosen, (2 * REACH + 1) * u + v]
                    * shifted[v, start : start + TILE_ROWS, :]
                )
        result[plane] = summed


def short_tables():
    index = np.arange(LANES)
    angle = 2.0 * np.pi * (index[:, None] * index[None, :] % LANES) / LANES
    cos, sin = np.cos(angle), np.sin(angle)
    table = np.block([[cos, -sin], [sin, cos]]).astype(np.float32)
    high = table.astype(BF16)
    low = (table - high.astype(np.float32)).astype(BF16)
    spin = 2.0 * np.pi * (np.arange(GROUPS)[:, None] * index[None, :]) / RANGE_BINS
    return high, low, np.cos(spin).astype(np.float32), np.sin(spin).astype(np.float32)


def shards(peers, swaths, *args):
    (polar, taps, weights, shifts, gains, owner, block_weights, kernel_index, bank) = args
    sections = taps.shape[0]
    vmem = pl.BlockSpec(memory_space=pltpu.VMEM)
    smem = pl.BlockSpec(memory_space=pltpu.SMEM)
    wide = pltpu.VMEM((ANGLES, GROUPS * WIDE), F32)
    tables = [jnp.asarray(t) for t in short_tables()]
    return pl.pallas_call(
        functools.partial(kernel, peers, swaths, sections),
        out_shape=jax.ShapeDtypeStruct((2, TILE_ROWS, LANES), F32),
        in_specs=[vmem] * 5 + [smem, vmem, smem, smem] + [vmem] * 4,
        out_specs=vmem,
        scratch_shapes=[
            pltpu.VMEM((GROUPS, TILE_ROWS, WIDE), F32),
            pltpu.VMEM((sections, 2, GROUPS, 2, ANGLES, LANES), F32),
            *([wide] * 9),
            pltpu.VMEM((ANGLES, ANGLES), F32),
            pltpu.VMEM((ANGLES, ANGLES), F32),
            pltpu.VMEM((2 * peers, TILE_ROWS, WIDE), F32),
            pltpu.VMEM((peers, TILE_ROWS, WIDE), F32),
            pltpu.VMEM((2, 3, EDGE, WIDE), F32),
            pltpu.VMEM((2, 2, EDGE, LANES), F32),
            pltpu.VMEM((2, LANES, TILE_ROWS), F32),
            pltpu.VMEM((2 * REACH + 1, TILE_ROWS + 2 * EDGE, LANES), F32),
            pltpu.SemaphoreType.DMA((sections, CHUNKS)),
            pltpu.SemaphoreType.DMA((sections, CHUNKS)),
            pltpu.SemaphoreType.DMA((2,)),
            pltpu.SemaphoreType.DMA((peers,)),
            pltpu.SemaphoreType.DMA((peers,)),
            pltpu.SemaphoreType.DMA((8,)),
            pltpu.SemaphoreType.DMA((8,)),
        ],
        compiler_params=pltpu.CompilerParams(
            collective_id=0, has_side_effects=True, vmem_limit_bytes=60 * 2**20
        ),
    )(
        polar,
        taps,
        weights,
        shifts,
        gains,
        owner.reshape(-1),
        block_weights,
        kernel_index.reshape(-1),
        bank,
        *tables,
    )


def solution(mesh):
    peers, swaths = mesh.shape["aper"], mesh.shape["swath"]
    in_specs = (
        P(None, "aper", "swath"),
        P(None, "aper", None, None, None),
        P(None, "aper", None, None, None),
        P(None, "aper", None, None),
        P(None, "swath"),
        P("aper", "swath", None, None),
        P("aper", "swath", None, None, None),
        P("aper", "swath"),
        P(),
    )
    return jax.shard_map(
        functools.partial(shards, peers, swaths),
        mesh=mesh,
        in_specs=in_specs,
        out_specs=P(None, "aper", "swath"),
        check_vma=False,
    )
```

```python
import functools
import math

import jax
import jax.numpy as jnp
import numpy as np
from jax import lax
from jax.experimental import pallas as pl
from jax.experimental.pallas import tpu as pltpu
from jax.sharding import PartitionSpec as P

ANGLES = 128
RANGE_BINS = 1024
LANES = 128
GROUPS = RANGE_BINS // LANES
WIDE = 2 * LANES
TILE_ROWS = 128
TAPS = 8
CHUNKS = 16
MIXES = 4
ROWS = ANGLES // CHUNKS
BLOCK = ANGLES // MIXES
EDGE = 8
REACH = 4
MESH = pl.DeviceIdType.MESH
F32 = jnp.float32
BF16 = jnp.bfloat16


def split(value):
    high = value.astype(BF16)
    return high, (value - high.astype(F32)).astype(BF16)


def product(left, right):
    def dot(a, b):
        return jnp.dot(a, b, preferred_element_type=F32)

    return dot(left[0], right[0]) + dot(left[1], right[0]) + dot(left[0], right[1])


def turn(value):
    half = (value - jnp.floor(value + 0.5)) * F32(math.pi)
    square = half * half
    sine = F32(-1.0 / math.factorial(15))
    for order in (13, 11, 9, 7, 5, 3, 1):
        sign = 1.0 if order % 4 == 1 else -1.0
        sine = sine * square + F32(sign / math.factorial(order))
    sine = sine * half
    cosine = F32(1.0 / math.factorial(16))
    for order in (14, 12, 10, 8, 6, 4, 2, 0):
        sign = 1.0 if order % 4 == 0 else -1.0
        cosine = cosine * square + F32(sign / math.factorial(order))
    return 1.0 - 2.0 * sine * sine, 2.0 * sine * cosine


def four(x):
    (ar, ai), (br, bi), (cr, ci), (dr, di) = x
    sr, si, tr, ti = ar + cr, ai + ci, ar - cr, ai - ci
    ur, ui, vr, vi = br + dr, bi + di, br - dr, bi - di
    return [(sr + ur, si + ui), (tr + vi, ti - vr), (sr - ur, si - ui), (tr - vi, ti + vr)]


def eight(x):
    even, odd = four(x[0::2]), four(x[1::2])
    root = F32(math.sqrt(0.5))
    turned = [
        odd[0],
        ((odd[1][0] + odd[1][1]) * root, (odd[1][1] - odd[1][0]) * root),
        (odd[2][1], -odd[2][0]),
        ((odd[3][1] - odd[3][0]) * root, -(odd[3][0] + odd[3][1]) * root),
    ]
    first = [(e[0] + o[0], e[1] + o[1]) for e, o in zip(even, turned)]
    return first + [(e[0] - o[0], e[1] - o[1]) for e, o in zip(even, turned)]


def twiddle(pairs, cos_ref, sin_ref):
    out = [pairs[0]]
    for group in range(1, GROUPS):
        a, b = pairs[group]
        c, s = cos_ref[group : group + 1, :], sin_ref[group : group + 1, :]
        out.append((a * c + b * s, b * c - a * s))
    return out


def short_dft(pairs, table):
    rows = pairs[0][0].shape[0]
    stacked = jnp.concatenate([jnp.concatenate(pair, axis=1) for pair in pairs], axis=0)
    out = product(split(stacked), table)
    return [out[g * rows : (g + 1) * rows] for g in range(len(pairs))]


def forward(pairs, table, cos_ref, sin_ref):
    return short_dft(twiddle(eight(pairs), cos_ref, sin_ref), table)


def inverse(merged, table, cos_ref, sin_ref, gain):
    out = short_dft([(im, re) for re, im in merged], table)
    pairs = eight(twiddle([(o[:, :LANES], o[:, LANES:]) for o in out], cos_ref, sin_ref))
    scaled = gain * F32(1.0 / RANGE_BINS)
    result = []
    for group, (im, re) in enumerate(pairs):
        weight = scaled[:, group * LANES : (group + 1) * LANES]
        result.append((re * weight, im * weight))
    return result


def kernel(
    peers,
    swaths,
    sections,
    polar_in,
    taps,
    weights,
    shifts,
    gains,
    owner,
    weights_in,
    kernel_index,
    bank,
    table_high,
    table_low,
    cos_ref,
    sin_ref,
    result,
    polar,
    block_weights,
    weights_high,
    weights_low,
    matrix,
    phases,
    spec0,
    spec1,
    spec2,
    got0,
    got1,
    got2,
    mixed,
    total,
    image,
    mat_send,
    mat_got,
    part,
    part_got,
    row_halo,
    col_halo,
    flipped,
    shifted,
    in_sem,
    send_sem,
    recv_sem,
    mat_sem,
    part_send,
    part_recv,
    halo_send,
    halo_recv,
):
    me = lax.axis_index("aper")
    column = lax.axis_index("swath")
    levels = peers.bit_length() - 1

    row_halo[...] = jnp.zeros_like(row_halo)
    col_halo[...] = jnp.zeros_like(col_halo)

    around = [(da, ds) for da in (-1, 0, 1) for ds in (-1, 0, 1) if (da, ds) != (0, 0)]
    barrier = pltpu.get_barrier_semaphore()
    for level in range(levels):
        pl.semaphore_signal(
            barrier, inc=1, device_id=(me ^ (1 << level), column), device_id_type=MESH
        )
    for da, ds in around:
        where = (lax.rem(me + da + peers, peers), lax.rem(column + ds + swaths, swaths))
        pl.semaphore_signal(barrier, inc=1, device_id=where, device_id_type=MESH)

    loads = [
        pltpu.make_async_copy(
            polar_in.at[:, pl.ds(k * BLOCK, BLOCK)],
            polar.at[:, pl.ds(k * BLOCK, BLOCK)],
            in_sem.at[k],
        )
        for k in range(MIXES)
    ]
    loads.append(pltpu.make_async_copy(weights_in.at[0, 0], block_weights, in_sem.at[MIXES]))
    for load in loads:
        load.start()

    bits = [lax.rem(me // (1 << step), 2) for step in range(levels)]
    table = (table_high[...], table_low[...])

    def interp(step, child):
        index = taps[step, 0, child]
        weight = weights[step, 0, child]
        rows = lax.broadcasted_iota(jnp.int32, (ANGLES, ANGLES), 0)
        built = jnp.zeros((ANGLES, ANGLES), F32)
        for tap in range(TAPS):
            built = built + jnp.where(
                index[tap : tap + 1, :] == rows, weight[tap : tap + 1, :], F32(0.0)
            )
        return built.T

    def fill_phases(step, side, child):
        row = shifts[step, 0, pl.ds(child, 1), :]
        shift = jnp.broadcast_to(row, (ANGLES, LANES)).T
        lane = lax.broadcasted_iota(jnp.int32, (ANGLES, LANES), 1)
        signed = jnp.where(lane < LANES // 2, lane, lane - LANES).astype(F32)
        unit = shift * F32(-1.0 / RANGE_BINS)
        step_cos, step_sin = turn(unit)
        a, b = turn(unit * (signed * F32(GROUPS)))
        for group in range(GROUPS):
            phases[step, side, group, 0] = a
            phases[step, side, group, 1] = b
            if group + 1 < GROUPS:
                a, b = a * step_cos - b * step_sin, b * step_cos + a * step_sin

    def steered(step, side, group, rows, value):
        a = phases[step, side, group, 0, rows, :]
        b = phases[step, side, group, 1, rows, :]
        re, im = value[:, :LANES], value[:, LANES:]
        return jnp.concatenate([a * re - b * im, b * re + a * im], axis=1)

    def lanes(group):
        return slice(group * WIDE, (group + 1) * WIDE)

    def chunk(k):
        return slice(k * ROWS, (k + 1) * ROWS)

    def block(k):
        return slice(k * BLOCK, (k + 1) * BLOCK)

    def inside(k):
        return range(k * CHUNKS // MIXES, (k + 1) * CHUNKS // MIXES)

    def exchange(step, k, source, target):
        return pltpu.make_async_remote_copy(
            src_ref=source.at[pl.ds(k * ROWS, ROWS)],
            dst_ref=target.at[pl.ds(k * ROWS, ROWS)],
            send_sem=send_sem.at[step, k],
            recv_sem=recv_sem.at[step, k],
            device_id=(me ^ (1 << step), column),
            device_id_type=MESH,
        )

    def store_wide(target, rows, values):
        for group in range(GROUPS):
            target[rows, lanes(group)] = values[group]

    def merged_rows(rows):
        pairs = []
        for group in range(GROUPS):
            value = total[rows, lanes(group)]
            pairs.append((value[:, :LANES], value[:, LANES:]))
        return pairs

    everything = slice(0, ANGLES)

    copies0 = []
    for k in range(MIXES):
        rows = block(k)
        loads[k].wait()
        pairs = [
            (polar[0, rows, g * LANES : (g + 1) * LANES], polar[1, rows, g * LANES : (g + 1) * LANES])
            for g in range(GROUPS)
        ]
        store_wide(spec0, rows, forward(pairs, table, cos_ref, sin_ref))
        if k == 0:
            pl.semaphore_wait(barrier, levels + len(around))
        for j in inside(k):
            copies0.append(exchange(0, j, spec0, got0))
            copies0[-1].start()
    mat_send[...] = interp(1, 1 - bits[1])
    mat_copy = pltpu.make_async_remote_copy(
        src_ref=mat_send,
        dst_ref=mat_got,
        send_sem=mat_sem.at[0],
        recv_sem=mat_sem.at[1],
        device_id=(me ^ 2, column),
        device_id_type=MESH,
    )
    mat_copy.start()
    fill_phases(0, 0, bits[0])
    fill_phases(0, 1, 1 - bits[0])

    def lefts_of(step):
        return [split(interp(step, child)) for child in (bits[step], 1 - bits[step])]

    lefts = {0: lefts_of(0)}

    def mix(step, side, source, first):
        left = lefts[step][side]
        for group in range(GROUPS):
            value = product(left, split(source[:, lanes(group)]))
            value = steered(step, side, group, everything, value)
            if not first:
                value = value + total[:, lanes(group)]
            total[:, lanes(group)] = value

    mix(0, 0, spec0, True)
    for copy in copies0:
        copy.wait()
    mix(0, 1, got0, False)
    for k in range(MIXES):
        rows = block(k)
        pairs = inverse(merged_rows(rows), table, cos_ref, sin_ref, gains[0:1, :])
        store_wide(spec1, rows, forward(pairs, table, cos_ref, sin_ref))

    mat_copy.wait()
    copies1 = []
    for k in range(MIXES):
        rows = block(k)
        left = split(mat_got[rows, :])
        for group in range(GROUPS):
            mixed[rows, lanes(group)] = product(left, split(spec1[:, lanes(group)]))
        for j in inside(k):
            copies1.append(exchange(1, j, mixed, got1))
            copies1[-1].start()
    lefts[1] = lefts_of(1)
    fill_phases(1, 0, bits[1])
    fill_phases(1, 1, 1 - bits[1])
    mix(1, 0, spec1, True)
    copies2 = []
    for k in range(CHUNKS):
        rows = chunk(k)
        copies1[k].wait()
        pairs = []
        for group in range(GROUPS):
            value = total[rows, lanes(group)] + steered(
                1, 1, group, rows, got1[rows, lanes(group)]
            )
            pairs.append((value[:, :LANES], value[:, LANES:]))
        pairs = inverse(pairs, table, cos_ref, sin_ref, gains[1:2, :])
        store_wide(spec2, rows, forward(pairs, table, cos_ref, sin_ref))
        copies2.append(exchange(2, k, spec2, got2))
        copies2[-1].start()
        if k == 0:
            fill_phases(2, 0, bits[2])
            fill_phases(2, 1, 1 - bits[2])
            lefts[2] = lefts_of(2)
            loads[MIXES].wait()
            for q in range(GROUPS):
                weights_high[q], weights_low[q] = split(block_weights[q])

    mix(2, 0, spec2, True)
    for copy in copies2:
        copy.wait()
    mix(2, 1, got2, False)
    for k in range(MIXES):
        rows = block(k)
        pairs = inverse(merged_rows(rows), table, cos_ref, sin_ref, gains[2:3, :])
        store_wide(image, rows, [jnp.concatenate(pair, axis=1) for pair in pairs])

    for q in range(GROUPS):
        matrix[q] = product((weights_high[q], weights_low[q]), split(image[:, lanes(q)]))

    def gathered(d):
        value = None
        for q in range(GROUPS):
            hit = jnp.where(owner[q] == d, F32(1.0), F32(0.0))
            value = hit * matrix[q] if value is None else value + hit * matrix[q]
        return value

    def part_copy(bit, half_at, slot, source, target):
        return pltpu.make_async_remote_copy(
            src_ref=source,
            dst_ref=target,
            send_sem=part_send.at[half_at, slot],
            recv_sem=part_recv.at[half_at, slot],
            device_id=(me ^ (1 << bit), column),
            device_id_type=MESH,
        )

    half = peers // 2
    copies = []
    for d in range(half):
        part[half + d] = gathered(2 * d + 1 - bits[0])
        copies.append(part_copy(0, 0, d, part.at[half + d], part_got.at[d]))
        copies[-1].start()
    for d in range(half):
        part[d] = gathered(2 * d + bits[0])
    for d in range(half):
        copies[d].wait()
        part[d] = part[d] + part_got[d]
    base, here = half, 0
    count = half
    cuts = [pl.ds(h * (TILE_ROWS // 2), TILE_ROWS // 2) for h in range(2)]
    for level in range(1, levels):
        count = count // 2
        copies = []
        for e in range(count):
            for h, cut in enumerate(cuts):
                bit = level if h == 0 else levels - level
                away = 1 - bits[bit]
                index = here + (2 * e + away if h == 0 else away * count + e)
                copy = part_copy(
                    bit, h, base + e, part.at[index, cut], part_got.at[base + e, cut]
                )
                copy.start()
                copies.append(copy)
        after = peers + base - half
        for e in range(count):
            for h, cut in enumerate(cuts):
                bit = level if h == 0 else levels - level
                index = here + (2 * e + bits[bit] if h == 0 else bits[bit] * count + e)
                copies[2 * e + h].wait()
                part[after + e, cut] = part[index, cut] + part_got[base + e, cut]
        here = after
        base = base + count
    tile = part.at[here]

    for plane in range(2):
        flipped[plane] = tile[:, plane * LANES : (plane + 1) * LANES].T

    def halo_copy(da, ds):
        slot = [r for r in range(len(around)) if around[r] == (-da, -ds)][0]
        if da != 0:
            edge = 0 if da < 0 else TILE_ROWS - EDGE
            source = tile.at[pl.ds(edge, EDGE)]
            target = row_halo.at[1 if da < 0 else 0, 1 - ds]
        else:
            edge = 0 if ds < 0 else LANES - EDGE
            source = flipped.at[:, pl.ds(edge, EDGE)]
            target = col_halo.at[1 if ds < 0 else 0]
        return pltpu.make_async_remote_copy(
            src_ref=source,
            dst_ref=target,
            send_sem=halo_send.at[slot],
            recv_sem=halo_recv.at[slot],
            device_id=(me + da, column + ds),
            device_id_type=MESH,
        )

    def present(da, ds):
        found = None
        for place, step, extent in ((me, da, peers), (column, ds, swaths)):
            if step != 0:
                inside = place > 0 if step < 0 else place < extent - 1
                found = inside if found is None else jnp.logical_and(found, inside)
        return found

    for da, ds in around:

        @pl.when(present(da, ds))
        def _(da=da, ds=ds):
            halo_copy(da, ds).start()

    for da, ds in around:

        @pl.when(present(da, ds))
        def _(da=da, ds=ds):
            halo_copy(da, ds).wait_send()
            halo_copy(-da, -ds).wait_recv()

    lane = lax.broadcasted_iota(jnp.int32, (EDGE, LANES), 1)
    chosen = kernel_index[0]
    gap = jnp.zeros((LANES - 2 * EDGE, LANES), F32)
    for plane in range(2):
        cut = slice(plane * LANES, (plane + 1) * LANES)

        def strip(end):
            side = jnp.where(
                lane < LANES // 2, row_halo[end, 2, :, cut], row_halo[end, 0, :, cut]
            )
            return jnp.concatenate([row_halo[end, 1, :, cut], side], axis=1)

        side = jnp.concatenate([col_halo[1, plane], gap, col_halo[0, plane]], axis=0).T
        middle = jnp.concatenate([tile[:, cut], side], axis=1)
        whole = jnp.concatenate([strip(0), middle, strip(1)], axis=0)
        summed = jnp.zeros((TILE_ROWS, LANES), F32)
        for v in range(2 * REACH + 1):
            moved = whole if v == REACH else pltpu.roll(whole, (REACH - v) % WIDE, 1)
            shifted[v] = moved[:, :LANES]
            for u in range(2 * REACH + 1):
                start = EDGE - REACH + u
                summed = (
                    summed
                    + bank[chosen, (2 * REACH + 1) * u + v]
                    * shifted[v, start : start + TILE_ROWS, :]
                )
        result[plane] = summed


def short_tables():
    index = np.arange(LANES)
    angle = 2.0 * np.pi * (index[:, None] * index[None, :] % LANES) / LANES
    cos, sin = np.cos(angle), np.sin(angle)
    table = np.block([[cos, -sin], [sin, cos]]).astype(np.float32)
    high = table.astype(BF16)
    low = (table - high.astype(np.float32)).astype(BF16)
    spin = 2.0 * np.pi * (np.arange(GROUPS)[:, None] * index[None, :]) / RANGE_BINS
    return high, low, np.cos(spin).astype(np.float32), np.sin(spin).astype(np.float32)


def shards(peers, swaths, *args):
    (polar, taps, weights, shifts, gains, owner, block_weights, kernel_index, bank) = args
    sections = taps.shape[0]
    vmem = pl.BlockSpec(memory_space=pltpu.VMEM)
    smem = pl.BlockSpec(memory_space=pltpu.SMEM)
    anywhere = pl.BlockSpec(memory_space=pl.ANY)
    wide = pltpu.VMEM((ANGLES, GROUPS * WIDE), F32)
    tables = [jnp.asarray(t) for t in short_tables()]
    return pl.pallas_call(
        functools.partial(kernel, peers, swaths, sections),
        out_shape=jax.ShapeDtypeStruct((2, TILE_ROWS, LANES), F32),
        in_specs=[anywhere] + [vmem] * 4 + [smem, anywhere, smem, smem] + [vmem] * 4,
        out_specs=vmem,
        scratch_shapes=[
            pltpu.VMEM(polar.shape, F32),
            pltpu.VMEM((GROUPS, TILE_ROWS, ANGLES), F32),
            pltpu.VMEM((GROUPS, TILE_ROWS, ANGLES), BF16),
            pltpu.VMEM((GROUPS, TILE_ROWS, ANGLES), BF16),
            pltpu.VMEM((GROUPS, TILE_ROWS, WIDE), F32),
            pltpu.VMEM((sections, 2, GROUPS, 2, ANGLES, LANES), F32),
            *([wide] * 9),
            pltpu.VMEM((ANGLES, ANGLES), F32),
            pltpu.VMEM((ANGLES, ANGLES), F32),
            pltpu.VMEM((2 * peers, TILE_ROWS, WIDE), F32),
            pltpu.VMEM((peers, TILE_ROWS, WIDE), F32),
            pltpu.VMEM((2, 3, EDGE, WIDE), F32),
            pltpu.VMEM((2, 2, EDGE, LANES), F32),
            pltpu.VMEM((2, LANES, TILE_ROWS), F32),
            pltpu.VMEM((2 * REACH + 1, TILE_ROWS + 2 * EDGE, LANES), F32),
            pltpu.SemaphoreType.DMA((MIXES + 1,)),
            pltpu.SemaphoreType.DMA((sections, CHUNKS)),
            pltpu.SemaphoreType.DMA((sections, CHUNKS)),
            pltpu.SemaphoreType.DMA((2,)),
            pltpu.SemaphoreType.DMA((2, peers)),
            pltpu.SemaphoreType.DMA((2, peers)),
            pltpu.SemaphoreType.DMA((8,)),
            pltpu.SemaphoreType.DMA((8,)),
        ],
        compiler_params=pltpu.CompilerParams(
            collective_id=0, has_side_effects=True, vmem_limit_bytes=60 * 2**20
        ),
    )(
        polar,
        taps,
        weights,
        shifts,
        gains,
        owner.reshape(-1),
        block_weights,
        kernel_index.reshape(-1),
        bank,
        *tables,
    )


def solution(mesh):
    peers, swaths = mesh.shape["aper"], mesh.shape["swath"]
    in_specs = (
        P(None, "aper", "swath"),
        P(None, "aper", None, None, None),
        P(None, "aper", None, None, None),
        P(None, "aper", None, None),
        P(None, "swath"),
        P("aper", "swath", None, None),
        P("aper", "swath", None, None, None),
        P("aper", "swath"),
        P(),
    )
    return jax.shard_map(
        functools.partial(shards, peers, swaths),
        mesh=mesh,
        in_specs=in_specs,
        out_specs=P(None, "aper", "swath"),
        check_vma=False,
    )
```

```python
import functools
import math

import jax
import jax.numpy as jnp
import numpy as np
from jax import lax
from jax.experimental import pallas as pl
from jax.experimental.pallas import tpu as pltpu
from jax.sharding import PartitionSpec as P

ANGLES = 128
RANGE_BINS = 1024
LANES = 128
GROUPS = RANGE_BINS // LANES
WIDE = 2 * LANES
TILE_ROWS = 128
TAPS = 8
CHUNKS = 16
MIXES = 4
ROWS = ANGLES // CHUNKS
BLOCK = ANGLES // MIXES
EDGE = 8
REACH = 4
MESH = pl.DeviceIdType.MESH
F32 = jnp.float32
BF16 = jnp.bfloat16


def split(value):
    high = value.astype(BF16)
    return high, (value - high.astype(F32)).astype(BF16)


def product(left, right):
    def dot(a, b):
        return jnp.dot(a, b, preferred_element_type=F32)

    return dot(left[0], right[0]) + dot(left[1], right[0]) + dot(left[0], right[1])


def turn(value):
    half = (value - jnp.floor(value + 0.5)) * F32(math.pi)
    square = half * half
    sine = F32(-1.0 / math.factorial(15))
    for order in (13, 11, 9, 7, 5, 3, 1):
        sign = 1.0 if order % 4 == 1 else -1.0
        sine = sine * square + F32(sign / math.factorial(order))
    sine = sine * half
    cosine = F32(1.0 / math.factorial(16))
    for order in (14, 12, 10, 8, 6, 4, 2, 0):
        sign = 1.0 if order % 4 == 0 else -1.0
        cosine = cosine * square + F32(sign / math.factorial(order))
    return 1.0 - 2.0 * sine * sine, 2.0 * sine * cosine


def four(x):
    (ar, ai), (br, bi), (cr, ci), (dr, di) = x
    sr, si, tr, ti = ar + cr, ai + ci, ar - cr, ai - ci
    ur, ui, vr, vi = br + dr, bi + di, br - dr, bi - di
    return [(sr + ur, si + ui), (tr + vi, ti - vr), (sr - ur, si - ui), (tr - vi, ti + vr)]


def eight(x):
    even, odd = four(x[0::2]), four(x[1::2])
    root = F32(math.sqrt(0.5))
    turned = [
        odd[0],
        ((odd[1][0] + odd[1][1]) * root, (odd[1][1] - odd[1][0]) * root),
        (odd[2][1], -odd[2][0]),
        ((odd[3][1] - odd[3][0]) * root, -(odd[3][0] + odd[3][1]) * root),
    ]
    first = [(e[0] + o[0], e[1] + o[1]) for e, o in zip(even, turned)]
    return first + [(e[0] - o[0], e[1] - o[1]) for e, o in zip(even, turned)]


def twiddle(pairs, cos_ref, sin_ref):
    out = [pairs[0]]
    for group in range(1, GROUPS):
        a, b = pairs[group]
        c, s = cos_ref[group : group + 1, :], sin_ref[group : group + 1, :]
        out.append((a * c + b * s, b * c - a * s))
    return out


def short_dft(pairs, table):
    rows = pairs[0][0].shape[0]
    stacked = jnp.concatenate([jnp.concatenate(pair, axis=1) for pair in pairs], axis=0)
    out = product(split(stacked), table)
    return [out[g * rows : (g + 1) * rows] for g in range(len(pairs))]


def forward(pairs, table, cos_ref, sin_ref):
    return short_dft(twiddle(eight(pairs), cos_ref, sin_ref), table)


def inverse(merged, table, cos_ref, sin_ref, gain):
    out = short_dft([(im, re) for re, im in merged], table)
    pairs = eight(twiddle([(o[:, :LANES], o[:, LANES:]) for o in out], cos_ref, sin_ref))
    scaled = gain * F32(1.0 / RANGE_BINS)
    result = []
    for group, (im, re) in enumerate(pairs):
        weight = scaled[:, group * LANES : (group + 1) * LANES]
        result.append((re * weight, im * weight))
    return result


def kernel(
    peers,
    swaths,
    sections,
    polar_in,
    taps,
    weights,
    shifts,
    gains,
    owner,
    weights_in,
    kernel_index,
    bank,
    table_high,
    table_low,
    cos_ref,
    sin_ref,
    result,
    polar,
    block_weights,
    weights_high,
    weights_low,
    matrix,
    phases,
    spec0,
    spec1,
    spec2,
    got0,
    got1,
    got2,
    mixed,
    total,
    image,
    mat_send,
    mat_got,
    part,
    part_got,
    row_halo,
    col_halo,
    flipped,
    shifted,
    in_sem,
    send_sem,
    recv_sem,
    mat_sem,
    part_send,
    part_recv,
    halo_send,
    halo_recv,
):
    me = lax.axis_index("aper")
    column = lax.axis_index("swath")
    levels = peers.bit_length() - 1

    row_halo[...] = jnp.zeros_like(row_halo)
    col_halo[...] = jnp.zeros_like(col_halo)

    around = [(da, ds) for da in (-1, 0, 1) for ds in (-1, 0, 1) if (da, ds) != (0, 0)]
    barrier = pltpu.get_barrier_semaphore()
    for level in range(levels):
        pl.semaphore_signal(
            barrier, inc=1, device_id=(me ^ (1 << level), column), device_id_type=MESH
        )
    for da, ds in around:
        where = (lax.rem(me + da + peers, peers), lax.rem(column + ds + swaths, swaths))
        pl.semaphore_signal(barrier, inc=1, device_id=where, device_id_type=MESH)

    loads = [
        pltpu.make_async_copy(
            polar_in.at[:, pl.ds(k * BLOCK, BLOCK)],
            polar.at[:, pl.ds(k * BLOCK, BLOCK)],
            in_sem.at[k],
        )
        for k in range(MIXES)
    ]
    loads.append(pltpu.make_async_copy(weights_in.at[0, 0], block_weights, in_sem.at[MIXES]))
    for load in loads:
        load.start()

    bits = [lax.rem(me // (1 << step), 2) for step in range(levels)]
    table = (table_high[...], table_low[...])

    def interp(step, child):
        index = taps[step, 0, child]
        weight = weights[step, 0, child]
        rows = lax.broadcasted_iota(jnp.int32, (ANGLES, ANGLES), 0)
        built = jnp.zeros((ANGLES, ANGLES), F32)
        for tap in range(TAPS):
            built = built + jnp.where(
                index[tap : tap + 1, :] == rows, weight[tap : tap + 1, :], F32(0.0)
            )
        return built.T

    def fill_phases(step, side, child):
        row = shifts[step, 0, pl.ds(child, 1), :]
        shift = jnp.broadcast_to(row, (ANGLES, LANES)).T
        lane = lax.broadcasted_iota(jnp.int32, (ANGLES, LANES), 1)
        signed = jnp.where(lane < LANES // 2, lane, lane - LANES).astype(F32)
        unit = shift * F32(-1.0 / RANGE_BINS)
        step_cos, step_sin = turn(unit)
        a, b = turn(unit * (signed * F32(GROUPS)))
        for group in range(GROUPS):
            phases[step, side, group, 0] = a
            phases[step, side, group, 1] = b
            if group + 1 < GROUPS:
                a, b = a * step_cos - b * step_sin, b * step_cos + a * step_sin

    def steered(step, side, group, rows, value):
        a = phases[step, side, group, 0, rows, :]
        b = phases[step, side, group, 1, rows, :]
        re, im = value[:, :LANES], value[:, LANES:]
        return jnp.concatenate([a * re - b * im, b * re + a * im], axis=1)

    def lanes(group):
        return slice(group * WIDE, (group + 1) * WIDE)

    def chunk(k):
        return slice(k * ROWS, (k + 1) * ROWS)

    def block(k):
        return slice(k * BLOCK, (k + 1) * BLOCK)

    def inside(k):
        return range(k * CHUNKS // MIXES, (k + 1) * CHUNKS // MIXES)

    def exchange(step, k, source, target):
        return pltpu.make_async_remote_copy(
            src_ref=source.at[pl.ds(k * ROWS, ROWS)],
            dst_ref=target.at[pl.ds(k * ROWS, ROWS)],
            send_sem=send_sem.at[step, k],
            recv_sem=recv_sem.at[step, k],
            device_id=(me ^ (1 << step), column),
            device_id_type=MESH,
        )

    def store_wide(target, rows, values):
        for group in range(GROUPS):
            target[rows, lanes(group)] = values[group]

    def merged_rows(rows):
        pairs = []
        for group in range(GROUPS):
            value = total[rows, lanes(group)]
            pairs.append((value[:, :LANES], value[:, LANES:]))
        return pairs

    everything = slice(0, ANGLES)

    fill_phases(0, 0, bits[0])
    fill_phases(0, 1, 1 - bits[0])
    mat_send[...] = interp(1, 1 - bits[1])

    def lefts_of(step):
        return [split(interp(step, child)) for child in (bits[step], 1 - bits[step])]

    lefts = {0: lefts_of(0)}
    copies0 = []
    for k in range(MIXES):
        rows = block(k)
        loads[k].wait()
        pairs = [
            (polar[0, rows, g * LANES : (g + 1) * LANES], polar[1, rows, g * LANES : (g + 1) * LANES])
            for g in range(GROUPS)
        ]
        store_wide(spec0, rows, forward(pairs, table, cos_ref, sin_ref))
        if k == 0:
            pl.semaphore_wait(barrier, levels + len(around))
        for j in inside(k):
            copies0.append(exchange(0, j, spec0, got0))
            copies0[-1].start()
    mat_copy = pltpu.make_async_remote_copy(
        src_ref=mat_send,
        dst_ref=mat_got,
        send_sem=mat_sem.at[0],
        recv_sem=mat_sem.at[1],
        device_id=(me ^ 2, column),
        device_id_type=MESH,
    )
    mat_copy.start()

    def mix(step, side, source, first):
        left = lefts[step][side]
        for group in range(GROUPS):
            value = product(left, split(source[:, lanes(group)]))
            value = steered(step, side, group, everything, value)
            if not first:
                value = value + total[:, lanes(group)]
            total[:, lanes(group)] = value

    mix(0, 0, spec0, True)
    for copy in copies0:
        copy.wait()
    mix(0, 1, got0, False)
    for k in range(MIXES):
        rows = block(k)
        pairs = inverse(merged_rows(rows), table, cos_ref, sin_ref, gains[0:1, :])
        store_wide(spec1, rows, forward(pairs, table, cos_ref, sin_ref))

    mat_copy.wait()
    copies1 = []
    for k in range(MIXES):
        rows = block(k)
        left = split(mat_got[rows, :])
        for group in range(GROUPS):
            mixed[rows, lanes(group)] = product(left, split(spec1[:, lanes(group)]))
        for j in inside(k):
            copies1.append(exchange(1, j, mixed, got1))
            copies1[-1].start()
    lefts[1] = lefts_of(1)
    fill_phases(1, 0, bits[1])
    fill_phases(1, 1, 1 - bits[1])
    mix(1, 0, spec1, True)
    copies2 = []
    for k in range(CHUNKS):
        rows = chunk(k)
        copies1[k].wait()
        pairs = []
        for group in range(GROUPS):
            value = total[rows, lanes(group)] + steered(
                1, 1, group, rows, got1[rows, lanes(group)]
            )
            pairs.append((value[:, :LANES], value[:, LANES:]))
        pairs = inverse(pairs, table, cos_ref, sin_ref, gains[1:2, :])
        store_wide(spec2, rows, forward(pairs, table, cos_ref, sin_ref))
        copies2.append(exchange(2, k, spec2, got2))
        copies2[-1].start()
        if k == 0:
            fill_phases(2, 0, bits[2])
            fill_phases(2, 1, 1 - bits[2])
            lefts[2] = lefts_of(2)
            loads[MIXES].wait()
            for q in range(GROUPS):
                weights_high[q], weights_low[q] = split(block_weights[q])

    mix(2, 0, spec2, True)
    for copy in copies2:
        copy.wait()
    mix(2, 1, got2, False)
    for k in range(MIXES):
        rows = block(k)
        pairs = inverse(merged_rows(rows), table, cos_ref, sin_ref, gains[2:3, :])
        store_wide(image, rows, [jnp.concatenate(pair, axis=1) for pair in pairs])

    for q in range(GROUPS):
        matrix[q] = product((weights_high[q], weights_low[q]), split(image[:, lanes(q)]))

    def gathered(d):
        value = None
        for q in range(GROUPS):
            hit = jnp.where(owner[q] == d, F32(1.0), F32(0.0))
            value = hit * matrix[q] if value is None else value + hit * matrix[q]
        return value

    def part_copy(bit, half_at, slot, source, target):
        return pltpu.make_async_remote_copy(
            src_ref=source,
            dst_ref=target,
            send_sem=part_send.at[half_at, slot],
            recv_sem=part_recv.at[half_at, slot],
            device_id=(me ^ (1 << bit), column),
            device_id_type=MESH,
        )

    half = peers // 2
    copies = []
    for d in range(half):
        part[half + d] = gathered(2 * d + 1 - bits[0])
        copies.append(part_copy(0, 0, d, part.at[half + d], part_got.at[d]))
        copies[-1].start()
    for d in range(half):
        part[d] = gathered(2 * d + bits[0])
    for d in range(half):
        copies[d].wait()
        part[d] = part[d] + part_got[d]
    base, here = half, 0
    count = half
    cuts = [pl.ds(h * (TILE_ROWS // 2), TILE_ROWS // 2) for h in range(2)]
    for level in range(1, levels):
        count = count // 2
        copies = []
        for e in range(count):
            for h, cut in enumerate(cuts):
                bit = level if h == 0 else levels - level
                away = 1 - bits[bit]
                index = here + (2 * e + away if h == 0 else away * count + e)
                copy = part_copy(
                    bit, h, base + e, part.at[index, cut], part_got.at[base + e, cut]
                )
                copy.start()
                copies.append(copy)
        after = peers + base - half
        for e in range(count):
            for h, cut in enumerate(cuts):
                bit = level if h == 0 else levels - level
                index = here + (2 * e + bits[bit] if h == 0 else bits[bit] * count + e)
                copies[2 * e + h].wait()
                part[after + e, cut] = part[index, cut] + part_got[base + e, cut]
        here = after
        base = base + count
    tile = part.at[here]

    for plane in range(2):
        flipped[plane] = tile[:, plane * LANES : (plane + 1) * LANES].T

    def halo_copy(da, ds):
        slot = [r for r in range(len(around)) if around[r] == (-da, -ds)][0]
        if da != 0:
            edge = 0 if da < 0 else TILE_ROWS - EDGE
            source = tile.at[pl.ds(edge, EDGE)]
            target = row_halo.at[1 if da < 0 else 0, 1 - ds]
        else:
            edge = 0 if ds < 0 else LANES - EDGE
            source = flipped.at[:, pl.ds(edge, EDGE)]
            target = col_halo.at[1 if ds < 0 else 0]
        return pltpu.make_async_remote_copy(
            src_ref=source,
            dst_ref=target,
            send_sem=halo_send.at[slot],
            recv_sem=halo_recv.at[slot],
            device_id=(me + da, column + ds),
            device_id_type=MESH,
        )

    def present(da, ds):
        found = None
        for place, step, extent in ((me, da, peers), (column, ds, swaths)):
            if step != 0:
                inside = place > 0 if step < 0 else place < extent - 1
                found = inside if found is None else jnp.logical_and(found, inside)
        return found

    for da, ds in around:

        @pl.when(present(da, ds))
        def _(da=da, ds=ds):
            halo_copy(da, ds).start()

    for da, ds in around:

        @pl.when(present(da, ds))
        def _(da=da, ds=ds):
            halo_copy(da, ds).wait_send()
            halo_copy(-da, -ds).wait_recv()

    lane = lax.broadcasted_iota(jnp.int32, (EDGE, LANES), 1)
    chosen = kernel_index[0]
    gap = jnp.zeros((LANES - 2 * EDGE, LANES), F32)
    for plane in range(2):
        cut = slice(plane * LANES, (plane + 1) * LANES)

        def strip(end):
            side = jnp.where(
                lane < LANES // 2, row_halo[end, 2, :, cut], row_halo[end, 0, :, cut]
            )
            return jnp.concatenate([row_halo[end, 1, :, cut], side], axis=1)

        side = jnp.concatenate([col_halo[1, plane], gap, col_halo[0, plane]], axis=0).T
        middle = jnp.concatenate([tile[:, cut], side], axis=1)
        whole = jnp.concatenate([strip(0), middle, strip(1)], axis=0)
        summed = jnp.zeros((TILE_ROWS, LANES), F32)
        for v in range(2 * REACH + 1):
            moved = whole if v == REACH else pltpu.roll(whole, (REACH - v) % WIDE, 1)
            shifted[v] = moved[:, :LANES]
            for u in range(2 * REACH + 1):
                start = EDGE - REACH + u
                summed = (
                    summed
                    + bank[chosen, (2 * REACH + 1) * u + v]
                    * shifted[v, start : start + TILE_ROWS, :]
                )
        result[plane] = summed


def short_tables():
    index = np.arange(LANES)
    angle = 2.0 * np.pi * (index[:, None] * index[None, :] % LANES) / LANES
    cos, sin = np.cos(angle), np.sin(angle)
    table = np.block([[cos, -sin], [sin, cos]]).astype(np.float32)
    high = table.astype(BF16)
    low = (table - high.astype(np.float32)).astype(BF16)
    spin = 2.0 * np.pi * (np.arange(GROUPS)[:, None] * index[None, :]) / RANGE_BINS
    return high, low, np.cos(spin).astype(np.float32), np.sin(spin).astype(np.float32)


def shards(peers, swaths, *args):
    (polar, taps, weights, shifts, gains, owner, block_weights, kernel_index, bank) = args
    sections = taps.shape[0]
    vmem = pl.BlockSpec(memory_space=pltpu.VMEM)
    smem = pl.BlockSpec(memory_space=pltpu.SMEM)
    anywhere = pl.BlockSpec(memory_space=pl.ANY)
    wide = pltpu.VMEM((ANGLES, GROUPS * WIDE), F32)
    tables = [jnp.asarray(t) for t in short_tables()]
    return pl.pallas_call(
        functools.partial(kernel, peers, swaths, sections),
        out_shape=jax.ShapeDtypeStruct((2, TILE_ROWS, LANES), F32),
        in_specs=[anywhere] + [vmem] * 4 + [smem, anywhere, smem, smem] + [vmem] * 4,
        out_specs=vmem,
        scratch_shapes=[
            pltpu.VMEM(polar.shape, F32),
            pltpu.VMEM((GROUPS, TILE_ROWS, ANGLES), F32),
            pltpu.VMEM((GROUPS, TILE_ROWS, ANGLES), BF16),
            pltpu.VMEM((GROUPS, TILE_ROWS, ANGLES), BF16),
            pltpu.VMEM((GROUPS, TILE_ROWS, WIDE), F32),
            pltpu.VMEM((sections, 2, GROUPS, 2, ANGLES, LANES), F32),
            *([wide] * 9),
            pltpu.VMEM((ANGLES, ANGLES), F32),
            pltpu.VMEM((ANGLES, ANGLES), F32),
            pltpu.VMEM((2 * peers, TILE_ROWS, WIDE), F32),
            pltpu.VMEM((peers, TILE_ROWS, WIDE), F32),
            pltpu.VMEM((2, 3, EDGE, WIDE), F32),
            pltpu.VMEM((2, 2, EDGE, LANES), F32),
            pltpu.VMEM((2, LANES, TILE_ROWS), F32),
            pltpu.VMEM((2 * REACH + 1, TILE_ROWS + 2 * EDGE, LANES), F32),
            pltpu.SemaphoreType.DMA((MIXES + 1,)),
            pltpu.SemaphoreType.DMA((sections, CHUNKS)),
            pltpu.SemaphoreType.DMA((sections, CHUNKS)),
            pltpu.SemaphoreType.DMA((2,)),
            pltpu.SemaphoreType.DMA((2, peers)),
            pltpu.SemaphoreType.DMA((2, peers)),
            pltpu.SemaphoreType.DMA((8,)),
            pltpu.SemaphoreType.DMA((8,)),
        ],
        compiler_params=pltpu.CompilerParams(
            collective_id=0, has_side_effects=True, vmem_limit_bytes=60 * 2**20
        ),
    )(
        polar,
        taps,
        weights,
        shifts,
        gains,
        owner.reshape(-1),
        block_weights,
        kernel_index.reshape(-1),
        bank,
        *tables,
    )


def solution(mesh):
    peers, swaths = mesh.shape["aper"], mesh.shape["swath"]
    in_specs = (
        P(None, "aper", "swath"),
        P(None, "aper", None, None, None),
        P(None, "aper", None, None, None),
        P(None, "aper", None, None),
        P(None, "swath"),
        P("aper", "swath", None, None),
        P("aper", "swath", None, None, None),
        P("aper", "swath"),
        P(),
    )
    return jax.shard_map(
        functools.partial(shards, peers, swaths),
        mesh=mesh,
        in_specs=in_specs,
        out_specs=P(None, "aper", "swath"),
        check_vma=False,
    )
```
